512 devices in a mesh: walk: 8 (over x, core), chol: 64 (over z, y).
Axes of the slice: x: 4, y: 4, z: 16, core: 2. Of those that a mesh axis runs over, the one named last changes fastest.
Arguments:
- walkers: bfloat16 [64, 2048, 256], P('walk', 'chol'), may hold values from -2.5 to 2.5
- trial: bfloat16 [2048, 256], P('chol'), may hold values from -1.05 to 1.05
- cholesky: bfloat16 [32, 2048, 2048], P(None, 'chol'), may hold values from -0.125 to 0.125
- rotated: bfloat16 [32, 2048, 256], P(None, 'chol'), may hold values from -0.09375 to 0.09375
- fields: float32 [64, 32], P('walk'), may hold values from -4 to 4
- source: int32 [64], replicated, may hold values from 0 to 63, as said below
Outputs:
- propagated: bfloat16 [64, 2048, 256], P('walk', 'chol')
- force_bias: float32 [64, 32], P('walk')
The draws below stay inside these ranges and needn't reach their ends.
Inputs may be any that keep to these rules, and one draw needn't show every extreme that they name: source is a permutation of the walkers. New slots g * 8 to (g + 1) * 8 - 1 form group g, as do the old walkers. Of the old walkers of one group at most 4 fill slots of any one new group, and in every draw some group sends exactly 4 to some group.
All inputs are finite; a program needn't handle non-finite values.
Results may differ from the reference program's by a relative error of at most 0.0051.
Values may be sent and summed in bfloat16 or wider, within the bound.
A program may use at most 128 MiB of HBM per device.

```python
import math
import jax
import jax.numpy as jnp
from jax import lax

M = 2048
N = 256
CHOL = 32
WG = 8
ITERS = 3
W = 64


def draw_walkers(key, part):
    subkeys = jax.random.split(jax.random.fold_in(key, 23), 2)
    diagonal = jnp.exp(jax.random.uniform(subkeys[0], (W, N), minval=-0.22, maxval=0.22))
    noise_draw = jnp.clip(jax.random.normal(subkeys[1], (W, M, N)), -5.0, 5.0)
    row_index = jnp.arange(M)[:, None]
    col_index = jnp.arange(N)[None, :]
    scales = jnp.where(row_index < N, 0.13 / math.sqrt(N), 0.5)
    identity = (row_index == col_index).astype(jnp.float32)
    values = noise_draw * scales[None] + identity[None] * diagonal[:, None, :]
    return values.astype(jnp.bfloat16)


def draw_trial(key, part):
    subkey = jax.random.fold_in(key, 37)
    noise_draw = jnp.clip(jax.random.normal(subkey, (M, N)), -4.0, 4.0)
    row_index = jnp.arange(M)[:, None]
    col_index = jnp.arange(N)[None, :]
    scales = jnp.where(row_index < N, 0.08 / math.sqrt(N), 0.54 / math.sqrt(N * (M - N)))
    identity = (row_index == col_index).astype(jnp.float32)
    return (identity + scales * noise_draw).astype(jnp.bfloat16)


def draw_source(key, part):
    groups = W // WG
    half_group = WG // 2
    subkeys = jax.random.split(jax.random.fold_in(key, 11), 4)
    first_dest = jax.random.permutation(subkeys[0], groups)
    rotation = jax.random.randint(subkeys[1], (), 1, groups)
    first_source = jnp.argsort(first_dest)
    second_source = (first_source - rotation) % groups
    orders = jax.vmap(lambda subkey: jax.random.permutation(subkey, WG))(jax.random.split(subkeys[2], groups))
    from_first = first_source[:, None] * WG + orders[first_source][:, :half_group]
    from_second = second_source[:, None] * WG + orders[second_source][:, half_group:]
    incoming = jnp.concatenate([from_first, from_second], axis=1)
    places = jax.vmap(lambda subkey: jax.random.permutation(subkey, WG))(jax.random.split(subkeys[3], groups))
    arranged = jnp.take_along_axis(incoming, places, axis=1)
    return arranged.reshape(W).astype(jnp.int32)


def block_levels(stream_key, shape, shards, smallest, top_value):
    level = 1.0
    for axis_at, shards_of in shards:
        steps = jax.random.uniform(jax.random.fold_in(jax.random.fold_in(stream_key, 6), axis_at), (shards_of,), jnp.float32, smallest / len(shards), top_value / len(shards))
        level = level * jnp.repeat(jnp.exp(steps), shape[axis_at] // shards_of).reshape((-1,) + (1,) * (len(shape) - 1 - axis_at))
    return level


def gaussian(key, extent, scale, limit, shards=(), kind=jnp.bfloat16):
    entries = scale * jax.random.normal(key, extent, jnp.float32)
    if shards:
        entries = entries * block_levels(key, extent, shards, -0.22, 0.18)
    return jnp.clip(entries, -limit, limit).astype(kind)


def setup_inputs(seed: int = 0) -> dict:
    arg_keys = jax.random.split(jax.random.key(seed), 7)
    return {
        "walkers": draw_walkers(jax.random.fold_in(arg_keys[6], 71), 0),
        "trial": draw_trial(jax.random.fold_in(arg_keys[6], 71), 0),
        "cholesky": gaussian(arg_keys[2], (CHOL, M, M), M ** -0.5, 0.125, ((1, 64),)),
        "rotated": gaussian(arg_keys[3], (CHOL, M, N), (M * N // 128) ** -0.5, 0.09375, ((1, 64),)),
        "fields": gaussian(arg_keys[4], (W, CHOL), 1.0, 4.0, ((0, 8),), jnp.float32),
        "source": draw_source(jax.random.fold_in(arg_keys[6], 71), 0),
    }


TAU_ROOT = 0.1


def newton_inverse(intersections):
    identity = jnp.eye(intersections.shape[-1], dtype=jnp.float32)
    estimate = jnp.broadcast_to(identity, intersections.shape)
    for sweep_index in range(ITERS):
        product = jnp.einsum("wij,wjk->wik", intersections, estimate, precision=lax.Precision.HIGHEST)
        estimate = jnp.einsum("wij,wjk->wik", estimate, 2.0 * identity - product, precision=lax.Precision.HIGHEST)
    return estimate


def reference(walkers, trial, cholesky, rotated, fields, source):
    migrated = jnp.take(walkers, source, axis=0)
    intersections = jnp.einsum("pi,wpj->wij", trial.astype(jnp.float32), migrated.astype(jnp.float32))
    inverse = newton_inverse(intersections).astype(jnp.bfloat16)
    greens = jnp.einsum("wpj,wji->wpi", migrated.astype(jnp.float32), inverse.astype(jnp.float32)).astype(jnp.bfloat16)
    force_bias = TAU_ROOT * jnp.einsum("lpi,wpi->wl", rotated.astype(jnp.float32), greens.astype(jnp.float32))
    shifted = (fields - force_bias).astype(jnp.bfloat16)
    flat_chol = cholesky.reshape(cholesky.shape[0], -1)

    def propagate(paired):
        walker, weights = paired
        potential = (TAU_ROOT * jnp.dot(weights[None, :], flat_chol, preferred_element_type=jnp.float32)).astype(jnp.bfloat16).reshape(M, M)
        first_term = jnp.dot(potential, walker, preferred_element_type=jnp.float32)
        second_term = jnp.dot(potential, first_term.astype(jnp.bfloat16), preferred_element_type=jnp.float32)
        return (walker.astype(jnp.float32) + first_term + 0.5 * second_term).astype(jnp.bfloat16)

    propagated = lax.map(propagate, (migrated, shifted))
    return propagated, force_bias
```

```python
import functools

import jax
import jax.numpy as jnp
from jax import lax
from jax.experimental import pallas as pl
from jax.experimental.pallas import tpu as pltpu
from jax.sharding import PartitionSpec as P

TAU_ROOT = 0.1
Y = 4
CHUNKS = 4
LEAD = 3
F32 = jnp.float32
BF16 = jnp.bfloat16


def split_dot(a, b):
    a_hi = a.astype(BF16)
    b_hi = b.astype(BF16)
    a_lo = (a - a_hi.astype(F32)).astype(BF16)
    b_lo = (b - b_hi.astype(F32)).astype(BF16)
    dot = functools.partial(jnp.dot, preferred_element_type=F32)
    return dot(a_hi, b_hi) + (dot(a_hi, b_lo) + dot(a_lo, b_hi))


def kernel(
    groups, depth,
    source, walkers, trial, fields, rotated, cholesky,
    propagated, force_bias,
    staged, arrived, migrated, trial_rows, trial_all, walker_all, overlap,
    greens_out, greens_in, rotated_here, chol_here, bias_out, bias_y, bias_sum, bias_z,
    mixing, pot_out, pot_in, first_all, first_f32, second, result_out, result_in,
    local_sem, mig_s, mig_r, ty_s, ty_r, wy_s, wy_r, rt_s, rt_r, rw_s, rw_r,
    g_s, g_r, fy_s, fy_r, fz_s, fz_r, p_s, p_r, rf_s, rf_r, o_s, o_r,
):
    per_group, rows, electrons = walkers.shape
    vectors = fields.shape[1]
    orbitals = depth * Y * rows
    capacity = per_group // 2
    mine = per_group // Y
    block = rows * Y
    half = depth // 2
    group = lax.axis_index("walk")
    place = lax.axis_index("chol")
    z = lax.div(place, Y)
    y = lax.rem(place, Y)

    def at_y(k):
        return z * Y + lax.rem(y + k, Y)

    def at_z(k):
        return lax.rem(z + k + depth, depth) * Y + y

    def send(src, dst, s_sem, r_sem, where):
        return pltpu.make_async_remote_copy(
            src_ref=src, dst_ref=dst, send_sem=s_sem, recv_sem=r_sem,
            device_id=where, device_id_type=pl.DeviceIdType.MESH,
        )

    chol_copy = pltpu.make_async_copy(cholesky, chol_here, local_sem.at[0])
    rot_copy = pltpu.make_async_copy(rotated, rotated_here, local_sem.at[1])
    chol_copy.start()
    rot_copy.start()

    barrier = pltpu.get_barrier_semaphore()
    for k in range(1, groups):
        pl.semaphore_signal(barrier, inc=1, device_id={"walk": lax.rem(group + k, groups)},
                            device_id_type=pl.DeviceIdType.MESH)
    for k in range(1, Y):
        pl.semaphore_signal(barrier, inc=1, device_id={"chol": at_y(k)},
                            device_id_type=pl.DeviceIdType.MESH)
    for k in range(1, depth):
        pl.semaphore_signal(barrier, inc=1, device_id={"chol": at_z(k)},
                            device_id_type=pl.DeviceIdType.MESH)

    def picks(dest):
        chosen = [jnp.int32(0)] * capacity
        count = jnp.int32(0)
        for s in range(per_group):
            src = source[dest * per_group + s]
            here = lax.div(src, per_group) == group
            slot = lax.rem(src, per_group)
            for c in range(capacity):
                chosen[c] = jnp.where(here & (count == c), slot, chosen[c])
            count = count + here.astype(jnp.int32)
        return chosen

    for k in range(1, groups):
        dest = lax.rem(group + k, groups)
        for c, pick in enumerate(picks(dest)):
            staged[k, c] = walkers[pick]
    for c, pick in enumerate(picks(group)):
        arrived[group * capacity + c] = walkers[pick]

    pl.semaphore_wait(barrier, groups + Y + depth - 3)

    def mig_copy(k):
        dest = lax.rem(group + k, groups)
        return send(staged.at[k], arrived.at[pl.ds(group * capacity, capacity)],
                    mig_s.at[k], mig_r.at[k], {"walk": dest})

    def mig_arrival(k):
        origin = lax.rem(group - k + groups, groups)
        return send(staged.at[k], arrived.at[pl.ds(origin * capacity, capacity)],
                    mig_s.at[k], mig_r.at[k], {"walk": origin})

    for k in range(1, groups):
        mig_copy(k).start()

    def of_y(k):
        return lax.rem(y - k + Y, Y)

    def rows_of(owner):
        return pl.ds(pl.multiple_of(owner * rows, rows), rows)

    def ty_copy(k, owner):
        return send(trial, trial_rows.at[rows_of(owner)], ty_s.at[k], ty_r.at[k],
                    {"chol": at_y(k)})

    for k in range(1, Y):
        ty_copy(k, y).start()
    trial_rows[rows_of(y)] = trial[...]
    for k in range(1, Y):
        ty_copy(k, of_y(k)).wait_recv()
    trial_all[z] = trial_rows[...].astype(F32).T.astype(BF16)

    def forward(k, s):
        return lax.rem(z - k * s + 2 * depth, depth)

    def block_rows(origin):
        return pl.ds(pl.multiple_of(origin * block, block), block)

    def rt_copy(d, s, arriving=False):
        k = 1 if d == 0 else -1
        origin = forward(k, s + 1 if arriving else s)
        return send(trial_all.at[origin], trial_all.at[origin], rt_s.at[d, s], rt_r.at[d, s],
                    {"chol": at_z(k)})

    def ring_copy(buffer, s_sem, r_sem, d, s, c, arriving=False):
        k = 1 if d == 0 else -1
        origin = forward(k, s + 1 if arriving else s)
        part = buffer.at[c, block_rows(origin)]
        return send(part, part, s_sem.at[d, s, c], r_sem.at[d, s, c], {"chol": at_z(k)})

    steps = (half, half - 1)

    def trial_step(s):
        for d in range(2):
            if s < steps[d]:
                rt_copy(d, s, True).wait_recv()
                if s + 1 < steps[d]:
                    rt_copy(d, s + 1).start()

    def ring_step(buffer, s_sem, r_sem, s):
        for c in range(mine):
            for d in range(2):
                if s < steps[d]:
                    ring_copy(buffer, s_sem, r_sem, d, s, c, True).wait_recv()
                    if s + 1 < steps[d]:
                        ring_copy(buffer, s_sem, r_sem, d, s + 1, c).start()

    def ring_end(buffer, s_sem, r_sem):
        for d in range(2):
            for s in range(steps[d]):
                for c in range(mine):
                    ring_copy(buffer, s_sem, r_sem, d, s, c).wait_send()

    for d in range(2):
        if steps[d] > 0:
            rt_copy(d, 0).start()
    for s in range(LEAD - 1):
        trial_step(s)

    for k in range(1, groups):
        mig_arrival(k).wait_recv()
    for k in range(per_group):
        src = source[group * per_group + k]
        origin = lax.div(src, per_group)
        rank = jnp.int32(0)
        for j in range(k):
            other = lax.div(source[group * per_group + j], per_group)
            rank = rank + (other == origin).astype(jnp.int32)
        migrated[k] = arrived[origin * capacity + rank]

    def own_rows(owner):
        start = pl.multiple_of(z * block + owner * rows, rows)
        return pl.ds(start, rows)

    def wy_copy(k, owner):
        to = lax.rem(y + k, Y)
        return send(migrated.at[pl.ds(to * mine, mine)], walker_all.at[:, own_rows(owner)],
                    wy_s.at[k], wy_r.at[k], {"chol": at_y(k)})

    for k in range(1, Y):
        wy_copy(k, y).start()
    for c in range(mine):
        walker_all[c, own_rows(y)] = migrated[y * mine + c]
    trial_step(LEAD - 1)
    for k in range(1, Y):
        wy_copy(k, of_y(k)).wait_recv()
    for c in range(mine):
        for d in range(2):
            if steps[d] > 0:
                ring_copy(walker_all, rw_s, rw_r, d, 0, c).start()

    def add_overlap(origin):
        for c in range(mine):
            overlap[c] += jnp.dot(trial_all[origin], walker_all[c, block_rows(origin)],
                                  preferred_element_type=F32)

    overlap[...] = jnp.zeros_like(overlap)
    add_overlap(z)
    for s in range(half):
        ring_step(walker_all, rw_s, rw_r, s)
        trial_step(s + LEAD)
        for d in range(2):
            if s < steps[d]:
                add_overlap(forward(1 if d == 0 else -1, s + 1))

    row_id = lax.broadcasted_iota(jnp.int32, (electrons, electrons), 0)
    col_id = lax.broadcasted_iota(jnp.int32, (electrons, electrons), 1)
    identity = (row_id == col_id).astype(F32)
    for c in range(mine):
        residual = identity - overlap[c]
        squared = split_dot(residual, residual)
        fourth = split_dot(squared, squared)
        low = identity + residual
        low = low + split_dot(low, squared)
        inverse = (low + split_dot(low, fourth)).astype(BF16)
        greens_out[c] = jnp.dot(walker_all[c, block_rows(z)], inverse,
                                preferred_element_type=F32).astype(BF16)

    def turn_copy(src, dst, s_sem, r_sem, k, owner):
        to = lax.rem(y + k, Y)
        return send(src.at[:, rows_of(to)], dst.at[pl.ds(owner * mine, mine)],
                    s_sem.at[k], r_sem.at[k], {"chol": at_y(k)})

    for k in range(1, Y):
        turn_copy(greens_out, greens_in, g_s, g_r, k, y).start()
    for c in range(mine):
        greens_in[y * mine + c] = greens_out[c, rows_of(y)]
    rot_copy.wait()
    for k in range(1, Y):
        turn_copy(greens_out, greens_in, g_s, g_r, k, of_y(k)).wait_recv()

    wide = vectors * rows
    spread = lax.dot_general(
        greens_in[...].reshape(per_group * rows, electrons), rotated_here[...],
        (((1,), (1,)), ((), ())), preferred_element_type=F32,
    )
    same_row = (lax.rem(lax.broadcasted_iota(jnp.int32, (per_group * rows, wide), 0), rows)
                == lax.rem(lax.broadcasted_iota(jnp.int32, (per_group * rows, wide), 1), rows))
    picked = jnp.where(same_row, spread, 0.0).reshape(per_group, rows, wide).sum(axis=1)
    lanes = bias_out.shape[1]
    fold = (lax.div(lax.broadcasted_iota(jnp.int32, (wide, lanes), 0), rows)
            == lax.broadcasted_iota(jnp.int32, (wide, lanes), 1)).astype(F32)
    bias_out[...] = jnp.dot(picked, fold, precision=lax.Precision.HIGHEST,
                            preferred_element_type=F32)

    def fy_copy(k, owner):
        return send(bias_out, bias_y.at[owner], fy_s.at[k], fy_r.at[k], {"chol": at_y(k)})

    for k in range(1, Y):
        fy_copy(k, y).start()
    bias_y[y] = bias_out[...]
    for k in range(1, Y):
        fy_copy(k, of_y(k)).wait_recv()
    bias_sum[...] = bias_y[...].sum(axis=0)

    def fz_copy(k, owner):
        return send(bias_sum, bias_z.at[owner], fz_s.at[k], fz_r.at[k], {"chol": at_z(k)})

    for k in range(1, depth):
        fz_copy(k, z).start()
    bias_z[z] = bias_sum[...]
    for k in range(1, depth):
        fz_copy(k, lax.rem(z - k + depth, depth)).wait_recv()
    total = TAU_ROOT * bias_z[...].sum(axis=0)[:, :vectors]
    force_bias[...] = total
    shifted = (fields[...] - total).astype(BF16)

    unfold = (lax.broadcasted_iota(jnp.int32, (vectors, wide), 0)
              == lax.div(lax.broadcasted_iota(jnp.int32, (vectors, wide), 1), rows)).astype(BF16)
    stretched = jnp.dot(shifted, unfold, preferred_element_type=F32)
    stretched = jnp.broadcast_to(stretched[:, None, :], (per_group, rows, wide))
    mixing[...] = jnp.where(same_row, stretched.reshape(per_group * rows, wide), 0.0).astype(BF16)

    chol_copy.wait()
    width = orbitals // CHUNKS

    def pot_copy(k, n, owner):
        to = lax.rem(y + k, Y)
        cols = pl.ds(pl.multiple_of(n * width, width), width)
        return send(pot_out.at[pl.ds(to * mine, mine), :, cols],
                    pot_in.at[:, rows_of(owner), cols],
                    p_s.at[k, n], p_r.at[k, n], {"chol": at_y(k)})

    def pot_step(n, carry):
        cols = pl.ds(pl.multiple_of(n * width, width), width)
        made = TAU_ROOT * jnp.dot(mixing[...], chol_here[:, cols], preferred_element_type=F32)
        pot_out[:, :, cols] = made.astype(BF16).reshape(per_group, rows, width)
        for k in range(1, Y):
            pot_copy(k, n, y).start()
        for c in range(mine):
            pot_in[c, rows_of(y), cols] = pot_out[y * mine + c, :, cols]
        return carry

    lax.fori_loop(0, CHUNKS, pot_step, 0)
    for n in range(CHUNKS):
        for k in range(1, Y):
            pot_copy(k, n, of_y(k)).wait_recv()

    for c in range(mine):
        made = jnp.dot(pot_in[c], walker_all[c], preferred_element_type=F32)
        first_f32[c] = made
        first_all[c, block_rows(z)] = made.astype(BF16)
        for d in range(2):
            if steps[d] > 0:
                ring_copy(first_all, rf_s, rf_r, d, 0, c).start()

    def add_second(origin):
        for c in range(mine):
            cols = pl.ds(pl.multiple_of(origin * block, block), block)
            second[c] += jnp.dot(pot_in[c, :, cols], first_all[c, block_rows(origin)],
                                 preferred_element_type=F32)

    second[...] = jnp.zeros_like(second)
    add_second(z)
    for s in range(half):
        ring_step(first_all, rf_s, rf_r, s)
        for d in range(2):
            if s < steps[d]:
                add_second(forward(1 if d == 0 else -1, s + 1))

    for c in range(mine):
        result_out[c] = (walker_all[c, block_rows(z)].astype(F32) + first_f32[c]
                         + 0.5 * second[c]).astype(BF16)
    for k in range(1, Y):
        turn_copy(result_out, result_in, o_s, o_r, k, y).start()
    for c in range(mine):
        result_in[y * mine + c] = result_out[c, rows_of(y)]

    for k in range(1, groups):
        mig_copy(k).wait_send()
    for k in range(1, Y):
        ty_copy(k, y).wait_send()
        wy_copy(k, y).wait_send()
        turn_copy(greens_out, greens_in, g_s, g_r, k, y).wait_send()
        fy_copy(k, y).wait_send()
        for n in range(CHUNKS):
            pot_copy(k, n, y).wait_send()
    for k in range(1, depth):
        fz_copy(k, z).wait_send()
    for d in range(2):
        for s in range(steps[d]):
            rt_copy(d, s).wait_send()
    ring_end(walker_all, rw_s, rw_r)
    ring_end(first_all, rf_s, rf_r)
    for k in range(1, Y):
        turn_copy(result_out, result_in, o_s, o_r, k, of_y(k)).wait_recv()
    for k in range(1, Y):
        turn_copy(result_out, result_in, o_s, o_r, k, y).wait_send()
    propagated[...] = result_in[...]


def shards(walkers, trial, cholesky, rotated, fields, source):
    per_group, rows, electrons = walkers.shape
    vectors = rotated.shape[0]
    groups = lax.axis_size("walk")
    depth = lax.axis_size("chol") // Y
    orbitals = cholesky.shape[2]
    capacity = per_group // 2
    mine = per_group // Y
    block = rows * Y
    half = depth // 2
    wide = vectors * rows
    lanes = 128
    vmem = pltpu.VMEM
    dma = pltpu.SemaphoreType.DMA
    scratch = [
        vmem((groups, capacity, rows, electrons), BF16),
        vmem((groups * capacity, rows, electrons), BF16),
        vmem((per_group, rows, electrons), BF16),
        vmem((block, electrons), BF16),
        vmem((depth, electrons, block), BF16),
        vmem((mine, orbitals, electrons), BF16),
        vmem((mine, electrons, electrons), F32),
        vmem((mine, block, electrons), BF16),
        vmem((per_group, rows, electrons), BF16),
        vmem((wide, electrons), BF16),
        vmem((wide, orbitals), BF16),
        vmem((per_group, lanes), F32),
        vmem((Y, per_group, lanes), F32),
        vmem((per_group, lanes), F32),
        vmem((depth, per_group, lanes), F32),
        vmem((per_group * rows, wide), BF16),
        vmem((per_group, rows, orbitals), BF16),
        vmem((mine, block, orbitals), BF16),
        vmem((mine, orbitals, electrons), BF16),
        vmem((mine, block, electrons), F32),
        vmem((mine, block, electrons), F32),
        vmem((mine, block, electrons), BF16),
        vmem((per_group, rows, electrons), BF16),
        dma((2,)),
        dma((groups,)), dma((groups,)),
        dma((Y,)), dma((Y,)), dma((Y,)), dma((Y,)),
        dma((2, half)), dma((2, half)),
        dma((2, half, mine)), dma((2, half, mine)),
        dma((Y,)), dma((Y,)), dma((Y,)), dma((Y,)),
        dma((depth,)), dma((depth,)),
        dma((Y, CHUNKS)), dma((Y, CHUNKS)),
        dma((2, half, mine)), dma((2, half, mine)),
        dma((Y,)), dma((Y,)),
    ]
    in_vmem = pl.BlockSpec(memory_space=pltpu.VMEM)
    anywhere = pl.BlockSpec(memory_space=pl.ANY)
    return pl.pallas_call(
        functools.partial(kernel, groups, depth),
        out_shape=(
            jax.ShapeDtypeStruct(walkers.shape, BF16),
            jax.ShapeDtypeStruct(fields.shape, F32),
        ),
        in_specs=[pl.BlockSpec(memory_space=pltpu.SMEM), in_vmem, in_vmem, in_vmem,
                  anywhere, anywhere],
        out_specs=(in_vmem, in_vmem),
        scratch_shapes=scratch,
        compiler_params=pltpu.CompilerParams(
            collective_id=0, has_side_effects=True, vmem_limit_bytes=50 * 1024 * 1024
        ),
    )(source, walkers, trial, fields, rotated.reshape(wide, electrons),
      cholesky.reshape(wide, orbitals))


def solution(mesh):
    placed = (
        P("walk", "chol", None),
        P("chol", None),
        P(None, "chol", None),
        P(None, "chol", None),
        P("walk", None),
        P(),
    )
    return jax.shard_map(
        shards,
        mesh=mesh,
        in_specs=placed,
        out_specs=(P("walk", "chol", None), P("walk", None)),
        check_vma=False,
    )
```

```python
import functools

import jax
import jax.numpy as jnp
from jax import lax
from jax.experimental import pallas as pl
from jax.experimental.pallas import tpu as pltpu
from jax.sharding import PartitionSpec as P

TAU_ROOT = 0.1
Y = 8
LINE = 4
CHUNKS = 2
SUB = 4
F32 = jnp.float32
BF16 = jnp.bfloat16


def split_dot(a, b):
    a_hi = a.astype(BF16)
    b_hi = b.astype(BF16)
    a_lo = (a - a_hi.astype(F32)).astype(BF16)
    b_lo = (b - b_hi.astype(F32)).astype(BF16)
    dot = functools.partial(jnp.dot, preferred_element_type=F32)
    return dot(a_hi, b_hi) + (dot(a_hi, b_lo) + dot(a_lo, b_hi))


def kernel(
    groups, depth,
    source_far, walkers_far, trial_far, fields_far, rotated, cholesky,
    propagated, force_bias,
    source, walkers, trial, fields, staged, arrived, migrated, trial_all, trial_turned, walker_all, overlap,
    greens_out, greens_in, rotated_here, chol_here, bias_out, bias_y, bias_sum, bias_z,
    mixing, pot_out, pot_in, first_all, first_f32, second, result_out, result_in,
    local_sem, mig_s, mig_r, tz_s, tz_r, tx_s, tx_r, wy_s, wy_r, rw_s, rw_r,
    g_s, g_r, fy_s, fy_r, fz_s, fz_r, p_s, p_r, rf_s, rf_r, o_s, o_r,
):
    per_group, rows, electrons = walkers.shape
    vectors = fields.shape[1]
    orbitals = depth * Y * rows
    capacity = per_group // 2
    mine = per_group // Y
    block = rows * Y
    half = depth // 2
    strip = rows // 2
    group = lax.axis_index("walk")
    place = lax.axis_index("chol")
    z = lax.div(place, Y)
    y = lax.rem(place, Y)

    def at_y(k):
        return z * Y + lax.rem(y + k, Y)

    floors = depth * Y // LINE
    floor = lax.div(place, LINE)
    seat = lax.rem(place, LINE)

    def at_floor(k):
        return lax.rem(floor + k + floors, floors) * LINE + seat

    def at_z(k):
        return lax.rem(z + k + depth, depth) * Y + y

    def send(src, dst, s_sem, r_sem, where):
        return pltpu.make_async_remote_copy(
            src_ref=src, dst_ref=dst, send_sem=s_sem, recv_sem=r_sem,
            device_id=where, device_id_type=pl.DeviceIdType.MESH,
        )

    source_copy = pltpu.make_async_copy(source_far, source, local_sem.at[2])
    walkers_copy = pltpu.make_async_copy(walkers_far, walkers, local_sem.at[3])
    trial_copy = pltpu.make_async_copy(trial_far, trial, local_sem.at[4])
    fields_copy = pltpu.make_async_copy(fields_far, fields, local_sem.at[5])
    sent = []

    def begin(copy):
        copy.start()
        sent.append(copy)

    chol_copy = pltpu.make_async_copy(cholesky, chol_here, local_sem.at[0])
    rot_copy = pltpu.make_async_copy(rotated, rotated_here, local_sem.at[1])
    for copy in (source_copy, walkers_copy, trial_copy, fields_copy, rot_copy, chol_copy):
        copy.start()

    barrier = pltpu.get_barrier_semaphore()
    for k in range(1, groups):
        pl.semaphore_signal(barrier, inc=1, device_id={"walk": lax.rem(group + k, groups)},
                            device_id_type=pl.DeviceIdType.MESH)
    for k in range(1, Y):
        pl.semaphore_signal(barrier, inc=1, device_id={"chol": at_y(k)},
                            device_id_type=pl.DeviceIdType.MESH)
    for k in (1, -1):
        pl.semaphore_signal(barrier, inc=1, device_id={"chol": at_z(k)},
                            device_id_type=pl.DeviceIdType.MESH)
        pl.semaphore_signal(barrier, inc=1, device_id={"chol": at_floor(k)},
                            device_id_type=pl.DeviceIdType.MESH)

    source_copy.wait()
    walkers_copy.wait()
    trial_copy.wait()
    fields_copy.wait()

    def picks(dest):
        chosen = [jnp.int32(0)] * capacity
        count = jnp.int32(0)
        for s in range(per_group):
            src = source[dest * per_group + s]
            here = lax.div(src, per_group) == group
            slot = lax.rem(src, per_group)
            for c in range(capacity):
                chosen[c] = jnp.where(here & (count == c), slot, chosen[c])
            count = count + here.astype(jnp.int32)
        return chosen

    for k in range(1, groups):
        dest = lax.rem(group + k, groups)
        for c, pick in enumerate(picks(dest)):
            staged[k, c] = walkers[pick]
    for c, pick in enumerate(picks(group)):
        arrived[group * capacity + c] = walkers[pick]

    pl.semaphore_wait(barrier, groups + Y + 2)

    def mig_copy(k):
        dest = lax.rem(group + k, groups)
        return send(staged.at[k], arrived.at[pl.ds(group * capacity, capacity)],
                    mig_s.at[k], mig_r.at[k], {"walk": dest})

    def mig_arrival(k):
        origin = lax.rem(group - k + groups, groups)
        return send(staged.at[k], arrived.at[pl.ds(origin * capacity, capacity)],
                    mig_s.at[k], mig_r.at[k], {"walk": origin})

    signs = (1, -1)
    reach = (floors // 2, floors // 2 - 1)

    def tz_copy(d, q, arriving=False):
        hop = 1 if q % 2 else 2
        origin = lax.rem(floor - signs[d] * (q if arriving else q - hop) + 2 * floors, floors)
        part = trial_all.at[origin, seat]
        return send(part, part, tz_s.at[d, q - 1], tz_r.at[d, q - 1],
                    {"chol": at_floor(signs[d] * hop)})

    def trial_round(r):
        for d in range(2):
            if r > 0 and 2 * r <= reach[d]:
                tz_copy(d, 2 * r, True).wait_recv()
            for q in (2 * r + 2, 2 * r + 1):
                if q <= reach[d]:
                    begin(tz_copy(d, q))

    rounds = (floors // 2 + 1) // 2

    def trial_rest():
        for d in range(2):
            for q in range(1, reach[d] + 1):
                if q % 2 or q >= 2 * rounds:
                    tz_copy(d, q, True).wait_recv()

    def tx_copy(k, owner):
        part = trial_all.at[:, owner]
        return send(part, part, tx_s.at[k], tx_r.at[k],
                    {"chol": floor * LINE + lax.rem(seat + k, LINE)})

    trial_all[floor, seat] = trial[...]
    trial_round(0)
    for k in range(1, groups):
        begin(mig_copy(k))
    trial_round(1)

    def of_y(k):
        return lax.rem(y - k + Y, Y)

    def rows_of(owner):
        return pl.ds(pl.multiple_of(owner * rows, rows), rows)

    def forward(k, s):
        return lax.rem(z - k * s + 2 * depth, depth)

    def block_rows(origin):
        return pl.ds(pl.multiple_of(origin * block, block), block)

    piece = block // SUB

    def last(d, p):
        return half if p % 2 == d else half - 1

    def walker_part(origin, c, p):
        return walker_all.at[c, pl.ds(pl.multiple_of(origin * block + p * piece, piece), piece)]

    def ring_copy(part_of, s_sem, r_sem, d, s, c, p, arriving=False):
        part = part_of(forward(signs[d], s + 1 if arriving else s), c, p)
        at = c * SUB + p
        return send(part, part, s_sem.at[d, s, at], r_sem.at[d, s, at],
                    {"chol": at_z(signs[d])})

    def ring_start(part_of, s_sem, r_sem, c, pieces):
        for p in pieces:
            for d in range(2):
                if last(d, p) > 0:
                    begin(ring_copy(part_of, s_sem, r_sem, d, 0, c, p))

    def ring_step(part_of, s_sem, r_sem, s, use):
        for c in range(mine):
            for p in range(SUB):
                for d in range(2):
                    if s < last(d, p):
                        ring_copy(part_of, s_sem, r_sem, d, s, c, p, True).wait_recv()
                        if s + 1 < last(d, p):
                            begin(ring_copy(part_of, s_sem, r_sem, d, s + 1, c, p))
            for d in range(2 if s < half - 1 else 1):
                use(d, s, c)

    for r in range(2, rounds - 1):
        trial_round(r)
    for k in range(1, groups):
        mig_arrival(k).wait_recv()
    for k in range(per_group):
        src = source[group * per_group + k]
        origin = lax.div(src, per_group)
        rank = jnp.int32(0)
        for j in range(k):
            other = lax.div(source[group * per_group + j], per_group)
            rank = rank + (other == origin).astype(jnp.int32)
        migrated[k] = arrived[origin * capacity + rank]

    def own_rows(owner):
        start = pl.multiple_of(z * block + owner * rows, rows)
        return pl.ds(start, rows)

    def wy_copy(k, owner):
        to = lax.rem(y + k, Y)
        return send(migrated.at[pl.ds(to * mine, mine)], walker_all.at[:, own_rows(owner)],
                    wy_s.at[k], wy_r.at[k], {"chol": at_y(k)})

    for k in range(1, Y):
        begin(wy_copy(k, y))
    for c in range(mine):
        walker_all[c, own_rows(y)] = migrated[y * mine + c]
    for r in range(max(rounds - 1, 2), rounds):
        trial_round(r)
    for k in range(1, Y):
        wy_copy(k, of_y(k)).wait_recv()
    for c in range(mine):
        ring_start(walker_part, rw_s, rw_r, c, range(SUB))
    trial_rest()
    for k in range(1, LINE):
        begin(tx_copy(k, seat))

    def turn_trial(o, carry):
        rows_here = trial_all[pl.ds(o * (Y // LINE), Y // LINE)].reshape(block, electrons)
        trial_turned[o] = rows_here.astype(F32).T.astype(BF16)
        return carry

    def trial_times(origin, c):
        return jnp.dot(trial_turned[origin], walker_all[c, block_rows(origin)],
                       preferred_element_type=F32)

    pending = []

    def add_overlap(d, s, c):
        if s < turn_at:
            pending.append((d, s, c))
        else:
            overlap[c] += trial_times(forward(signs[d], s + 1), c)

    turn_at = min(2, half - 1)
    for s in range(half):
        if s == turn_at:
            for k in range(1, LINE):
                tx_copy(k, lax.rem(seat - k + LINE, LINE)).wait_recv()
            lax.fori_loop(0, depth, turn_trial, 0)
            for c in range(mine):
                overlap[c] = trial_times(z, c)
            for d, before, c in pending:
                overlap[c] += trial_times(forward(signs[d], before + 1), c)
        ring_step(walker_part, rw_s, rw_r, s, add_overlap)

    row_id = lax.broadcasted_iota(jnp.int32, (electrons, electrons), 0)
    col_id = lax.broadcasted_iota(jnp.int32, (electrons, electrons), 1)
    identity = (row_id == col_id).astype(F32)
    for c in range(mine):
        residual = identity - overlap[c]
        squared = split_dot(residual, residual)
        fourth = split_dot(squared, squared)
        low = identity + residual
        low = low + split_dot(low, squared)
        inverse = (low + split_dot(low, fourth)).astype(BF16)
        made = jnp.dot(walker_all[c, block_rows(z)], inverse, preferred_element_type=F32)
        greens_out[c] = made.astype(BF16).reshape(Y, rows, electrons)

    def turn_copy(src, dst, s_sem, r_sem, k, owner):
        to = lax.rem(y + k, Y)
        return send(src.at[:, to], dst.at[pl.ds(owner * mine, mine)],
                    s_sem.at[k], r_sem.at[k], {"chol": at_y(k)})

    for k in range(1, Y):
        begin(turn_copy(greens_out, greens_in, g_s, g_r, k, y))
    for c in range(mine):
        greens_in[y * mine + c] = greens_out[c, y]
    rot_copy.wait()
    for k in range(1, Y):
        turn_copy(greens_out, greens_in, g_s, g_r, k, of_y(k)).wait_recv()

    wide = vectors * rows
    spread = lax.dot_general(
        greens_in[...].reshape(per_group * rows, electrons), rotated_here[...],
        (((1,), (1,)), ((), ())), preferred_element_type=F32,
    )
    same_row = (lax.rem(lax.broadcasted_iota(jnp.int32, (per_group * rows, wide), 0), rows)
                == lax.rem(lax.broadcasted_iota(jnp.int32, (per_group * rows, wide), 1), rows))
    picked = jnp.where(same_row, spread, 0.0).reshape(per_group, rows, wide).sum(axis=1)
    lanes = bias_out.shape[1]
    fold = (lax.div(lax.broadcasted_iota(jnp.int32, (wide, lanes), 0), rows)
            == lax.broadcasted_iota(jnp.int32, (wide, lanes), 1)).astype(F32)
    bias_out[...] = jnp.dot(picked, fold, precision=lax.Precision.HIGHEST,
                            preferred_element_type=F32)

    def fy_copy(k, owner):
        return send(bias_out, bias_y.at[owner], fy_s.at[k], fy_r.at[k], {"chol": at_y(k)})

    for k in range(1, Y):
        begin(fy_copy(k, y))
    bias_y[y] = bias_out[...]
    for k in range(1, Y):
        fy_copy(k, of_y(k)).wait_recv()
    bias_sum[...] = bias_y[...].sum(axis=0)

    def fz_copy(k, owner):
        return send(bias_sum, bias_z.at[owner], fz_s.at[k], fz_r.at[k], {"chol": at_z(k)})

    for k in range(1, depth):
        begin(fz_copy(k, z))
    bias_z[z] = bias_sum[...]
    for k in range(1, depth):
        fz_copy(k, lax.rem(z - k + depth, depth)).wait_recv()
    total = TAU_ROOT * bias_z[...].sum(axis=0)[:, :vectors]
    force_bias[...] = total
    shifted = (fields[...] - total).astype(BF16)

    span = vectors * strip
    unfold = (lax.broadcasted_iota(jnp.int32, (vectors, span), 0)
              == lax.div(lax.broadcasted_iota(jnp.int32, (vectors, span), 1), strip)).astype(BF16)
    stretched = jnp.dot(shifted, unfold, preferred_element_type=F32)
    stretched = jnp.broadcast_to(stretched[:, None, :], (per_group, strip, span))
    kept = (lax.rem(lax.broadcasted_iota(jnp.int32, (per_group * strip, span), 0), strip)
            == lax.rem(lax.broadcasted_iota(jnp.int32, (per_group * strip, span), 1), strip))
    mixing[...] = jnp.where(kept, stretched.reshape(per_group * strip, span), 0.0).astype(BF16)

    chol_copy.wait()
    width = orbitals // CHUNKS

    def pot_copy(k, h, n, owner):
        to = lax.rem(y + k, Y)
        cols = pl.ds(n * width, width)
        return send(pot_out.at[h, pl.ds(to * mine, mine), :, cols],
                    pot_in.at[:, h, owner, :, cols],
                    p_s.at[k, h, n], p_r.at[k, h, n], {"chol": at_y(k)})

    for h in range(2):
        for n in range(CHUNKS):
            cols = pl.ds(n * width, width)
            side = chol_here[:, pl.ds(h * strip, strip), cols].reshape(span, width)
            made = TAU_ROOT * jnp.dot(mixing[...], side, preferred_element_type=F32)
            pot_out[h, :, :, cols] = made.astype(BF16).reshape(per_group, strip, width)
            for k in range(1, Y):
                begin(pot_copy(k, h, n, y))
            for c in range(mine):
                pot_in[c, h, y, :, cols] = pot_out[h, y * mine + c, :, cols]

    def first_part(origin, c, p):
        h, q = p // (SUB // 2), p % (SUB // 2)
        seats = Y // (SUB // 2)
        return first_all.at[c, origin, pl.ds(q * seats, seats), pl.ds(h * strip, strip)]

    for h in range(2):
        for n in range(CHUNKS):
            for k in range(1, Y):
                pot_copy(k, h, n, of_y(k)).wait_recv()
        for c in range(mine):
            made = jnp.dot(pot_in[c, h].reshape(Y * strip, orbitals), walker_all[c],
                           preferred_element_type=F32)
            first_f32[c, h] = made
            first_all[c, z, :, pl.ds(h * strip, strip)] = (
                made.astype(BF16).reshape(Y, strip, electrons))
            ring_start(first_part, rf_s, rf_r, c, range(h * (SUB // 2), (h + 1) * (SUB // 2)))

    def potential_times(origin, c):
        cols = pl.ds(pl.multiple_of(origin * block, block), block)
        return jnp.dot(pot_in[c, :, :, :, cols].reshape(block, block),
                       first_all[c, origin].reshape(block, electrons),
                       preferred_element_type=F32)

    def add_second(d, s, c):
        second[c] += potential_times(forward(signs[d], s + 1), c)

    for c in range(mine):
        second[c] = potential_times(z, c)
    for s in range(half):
        ring_step(first_part, rf_s, rf_r, s, add_second)

    for c in range(mine):
        own = walker_all[c, block_rows(z)].reshape(Y, rows, electrons)
        for h in range(2):
            low = own[:, h * strip:(h + 1) * strip].reshape(Y * strip, electrons).astype(F32)
            made = low + first_f32[c, h] + 0.5 * second[c, pl.ds(h * Y * strip, Y * strip)]
            result_out[c, :, pl.ds(h * strip, strip)] = (
                made.astype(BF16).reshape(Y, strip, electrons))
    for k in range(1, Y):
        begin(turn_copy(result_out, result_in, o_s, o_r, k, y))
    for c in range(mine):
        result_in[y * mine + c] = result_out[c, y]

    for k in range(1, Y):
        turn_copy(result_out, result_in, o_s, o_r, k, of_y(k)).wait_recv()
    for copy in sent:
        copy.wait_send()
    propagated[...] = result_in[...]


def shards(walkers, trial, cholesky, rotated, fields, source):
    per_group, rows, electrons = walkers.shape
    vectors = rotated.shape[0]
    groups = lax.axis_size("walk")
    depth = lax.axis_size("chol") // Y
    orbitals = cholesky.shape[2]
    capacity = per_group // 2
    mine = per_group // Y
    block = rows * Y
    half = depth // 2
    strip = rows // 2
    wide = vectors * rows
    lanes = 128
    vmem = pltpu.VMEM
    dma = pltpu.SemaphoreType.DMA
    scratch = [
        pltpu.SMEM(source.shape, jnp.int32),
        vmem(walkers.shape, BF16),
        vmem(trial.shape, BF16),
        vmem(fields.shape, F32),
        vmem((groups, capacity, rows, electrons), BF16),
        vmem((groups * capacity, rows, electrons), BF16),
        vmem((per_group, rows, electrons), BF16),
        vmem((depth * Y // LINE, LINE, rows, electrons), BF16),
        vmem((depth, electrons, block), BF16),
        vmem((mine, orbitals, electrons), BF16),
        vmem((mine, electrons, electrons), F32),
        vmem((mine, Y, rows, electrons), BF16),
        vmem((per_group, rows, electrons), BF16),
        vmem((wide, electrons), BF16),
        vmem((vectors, rows, orbitals), BF16),
        vmem((per_group, lanes), F32),
        vmem((Y, per_group, lanes), F32),
        vmem((per_group, lanes), F32),
        vmem((depth, per_group, lanes), F32),
        vmem((per_group * strip, vectors * strip), BF16),
        vmem((2, per_group, strip, orbitals), BF16),
        vmem((mine, 2, Y, strip, orbitals), BF16),
        vmem((mine, depth, Y, rows, electrons), BF16),
        vmem((mine, 2, Y * strip, electrons), F32),
        vmem((mine, block, electrons), F32),
        vmem((mine, Y, rows, electrons), BF16),
        vmem((per_group, rows, electrons), BF16),
        dma((6,)),
        dma((groups,)), dma((groups,)),
        dma((2, depth * Y // LINE // 2)), dma((2, depth * Y // LINE // 2)),
        dma((LINE,)), dma((LINE,)),
        dma((Y,)), dma((Y,)),
        dma((2, half, mine * SUB)), dma((2, half, mine * SUB)),
        dma((Y,)), dma((Y,)), dma((Y,)), dma((Y,)),
        dma((depth,)), dma((depth,)),
        dma((Y, 2, CHUNKS)), dma((Y, 2, CHUNKS)),
        dma((2, half, mine * SUB)), dma((2, half, mine * SUB)),
        dma((Y,)), dma((Y,)),
    ]
    in_vmem = pl.BlockSpec(memory_space=pltpu.VMEM)
    in_hbm = pl.BlockSpec(memory_space=pltpu.HBM)
    return pl.pallas_call(
        functools.partial(kernel, groups, depth),
        out_shape=(
            jax.ShapeDtypeStruct(walkers.shape, BF16),
            jax.ShapeDtypeStruct(fields.shape, F32),
        ),
        in_specs=[in_hbm] * 6,
        out_specs=(in_vmem, in_vmem),
        scratch_shapes=scratch,
        compiler_params=pltpu.CompilerParams(
            collective_id=0, has_side_effects=True, vmem_limit_bytes=67043328
        ),
    )(source, walkers, trial, fields, rotated.reshape(wide, electrons),
      cholesky)


def solution(mesh):
    placed = (
        P("walk", "chol", None),
        P("chol", None),
        P(None, "chol", None),
        P(None, "chol", None),
        P("walk", None),
        P(),
    )
    return jax.shard_map(
        shards,
        mesh=mesh,
        in_specs=placed,
        out_specs=(P("walk", "chol", None), P("walk", None)),
        check_vma=False,
    )
```

```python
import functools

import jax
import jax.numpy as jnp
from jax import lax
from jax.experimental import pallas as pl
from jax.experimental.pallas import tpu as pltpu
from jax.sharding import PartitionSpec as P

TAU_ROOT = 0.1
Y = 8
LINE = 4
CHUNKS = 2
SUB = 4
F32 = jnp.float32
BF16 = jnp.bfloat16


def split_dot(a, b):
    a_hi = a.astype(BF16)
    b_hi = b.astype(BF16)
    a_lo = (a - a_hi.astype(F32)).astype(BF16)
    b_lo = (b - b_hi.astype(F32)).astype(BF16)
    dot = functools.partial(jnp.dot, preferred_element_type=F32)
    return dot(a_hi, b_hi) + (dot(a_hi, b_lo) + dot(a_lo, b_hi))


def kernel(
    groups, depth,
    source_far, walkers_far, trial_far, fields_far, rotated, cholesky,
    propagated, force_bias,
    source, walkers, trial, fields, staged, arrived, migrated, trial_all, trial_turned, walker_all, overlap,
    greens_out, greens_in, rotated_here, chol_here, bias_out, bias_y, bias_sum, bias_z,
    mixing, pot_out, pot_in, first_all, first_f32, second, result_out, result_in,
    local_sem, mig_s, mig_r, tz_s, tz_r, tx_s, tx_r, wy_s, wy_r, rw_s, rw_r,
    g_s, g_r, fy_s, fy_r, fz_s, fz_r, p_s, p_r, rf_s, rf_r, o_s, o_r,
):
    per_group, rows, electrons = walkers.shape
    vectors = fields.shape[1]
    orbitals = depth * Y * rows
    capacity = per_group // 2
    mine = per_group // Y
    block = rows * Y
    half = depth // 2
    strip = rows // 2
    group = lax.axis_index("walk")
    place = lax.axis_index("chol")
    z = lax.div(place, Y)
    y = lax.rem(place, Y)

    def at_y(k):
        return z * Y + lax.rem(y + k, Y)

    floors = depth * Y // LINE
    floor = lax.div(place, LINE)
    seat = lax.rem(place, LINE)

    def at_floor(k):
        return lax.rem(floor + k + floors, floors) * LINE + seat

    def at_z(k):
        return lax.rem(z + k + depth, depth) * Y + y

    def send(src, dst, s_sem, r_sem, where):
        return pltpu.make_async_remote_copy(
            src_ref=src, dst_ref=dst, send_sem=s_sem, recv_sem=r_sem,
            device_id=where, device_id_type=pl.DeviceIdType.MESH,
        )

    source_copy = pltpu.make_async_copy(source_far, source, local_sem.at[2])
    walkers_copy = pltpu.make_async_copy(walkers_far, walkers, local_sem.at[3])
    trial_copy = pltpu.make_async_copy(trial_far, trial, local_sem.at[4])
    fields_copy = pltpu.make_async_copy(fields_far, fields, local_sem.at[5])
    sent = []

    def begin(copy):
        copy.start()
        sent.append(copy)

    chol_copy = pltpu.make_async_copy(cholesky, chol_here, local_sem.at[0])
    rot_copy = pltpu.make_async_copy(rotated, rotated_here, local_sem.at[1])
    for copy in (source_copy, walkers_copy, trial_copy, fields_copy, rot_copy, chol_copy):
        copy.start()

    barrier = pltpu.get_barrier_semaphore()
    for k in range(1, groups):
        pl.semaphore_signal(barrier, inc=1, device_id={"walk": lax.rem(group + k, groups)},
                            device_id_type=pl.DeviceIdType.MESH)
    for k in range(1, Y):
        pl.semaphore_signal(barrier, inc=1, device_id={"chol": at_y(k)},
                            device_id_type=pl.DeviceIdType.MESH)
    for k in (1, -1):
        pl.semaphore_signal(barrier, inc=1, device_id={"chol": at_z(k)},
                            device_id_type=pl.DeviceIdType.MESH)
        pl.semaphore_signal(barrier, inc=1, device_id={"chol": at_floor(k)},
                            device_id_type=pl.DeviceIdType.MESH)

    source_copy.wait()
    walkers_copy.wait()
    trial_copy.wait()
    fields_copy.wait()

    def picks(dest):
        chosen = [jnp.int32(0)] * capacity
        count = jnp.int32(0)
        for s in range(per_group):
            src = source[dest * per_group + s]
            here = lax.div(src, per_group) == group
            slot = lax.rem(src, per_group)
            for c in range(capacity):
                chosen[c] = jnp.where(here & (count == c), slot, chosen[c])
            count = count + here.astype(jnp.int32)
        return chosen

    for k in range(1, groups):
        dest = lax.rem(group + k, groups)
        for c, pick in enumerate(picks(dest)):
            staged[k, c] = walkers[pick]
    for c, pick in enumerate(picks(group)):
        arrived[group * capacity + c] = walkers[pick]

    pl.semaphore_wait(barrier, groups + Y + 2)

    def mig_copy(k):
        dest = lax.rem(group + k, groups)
        return send(staged.at[k], arrived.at[pl.ds(group * capacity, capacity)],
                    mig_s.at[k], mig_r.at[k], {"walk": dest})

    def mig_arrival(k):
        origin = lax.rem(group - k + groups, groups)
        return send(staged.at[k], arrived.at[pl.ds(origin * capacity, capacity)],
                    mig_s.at[k], mig_r.at[k], {"walk": origin})

    signs = (1, -1)
    reach = (floors // 2, floors // 2 - 1)

    def tz_copy(d, q, arriving=False):
        hop = 1 if q % 2 else 2
        origin = lax.rem(floor - signs[d] * (q if arriving else q - hop) + 2 * floors, floors)
        part = trial_all.at[origin, seat]
        return send(part, part, tz_s.at[d, q - 1], tz_r.at[d, q - 1],
                    {"chol": at_floor(signs[d] * hop)})

    def trial_round(r):
        for d in range(2):
            if r > 0 and 2 * r <= reach[d]:
                tz_copy(d, 2 * r, True).wait_recv()
            for q in (2 * r + 2, 2 * r + 1):
                if q <= reach[d]:
                    begin(tz_copy(d, q))

    rounds = (floors // 2 + 1) // 2

    def trial_rest():
        for d in range(2):
            for q in range(1, reach[d] + 1):
                if q % 2 or q >= 2 * rounds:
                    tz_copy(d, q, True).wait_recv()

    def tx_copy(k, owner):
        part = trial_all.at[:, owner]
        return send(part, part, tx_s.at[k], tx_r.at[k],
                    {"chol": floor * LINE + lax.rem(seat + k, LINE)})

    trial_all[floor, seat] = trial[...]
    trial_round(0)
    for k in range(1, groups):
        begin(mig_copy(k))
    trial_round(1)

    def of_y(k):
        return lax.rem(y - k + Y, Y)

    def rows_of(owner):
        return pl.ds(pl.multiple_of(owner * rows, rows), rows)

    def forward(k, s):
        return lax.rem(z - k * s + 2 * depth, depth)

    def block_rows(origin):
        return pl.ds(pl.multiple_of(origin * block, block), block)

    piece = block // SUB

    def last(d, p):
        return half if p % 2 == d else half - 1

    def walker_part(origin, c, p):
        return walker_all.at[c, pl.ds(pl.multiple_of(origin * block + p * piece, piece), piece)]

    def ring_copy(part_of, s_sem, r_sem, d, s, c, p, arriving=False):
        part = part_of(forward(signs[d], s + 1 if arriving else s), c, p)
        at = c * SUB + p
        return send(part, part, s_sem.at[d, s, at], r_sem.at[d, s, at],
                    {"chol": at_z(signs[d])})

    def ring_start(part_of, s_sem, r_sem, c, pieces):
        for p in pieces:
            for d in range(2):
                if last(d, p) > 0:
                    begin(ring_copy(part_of, s_sem, r_sem, d, 0, c, p))

    def ring_step(part_of, s_sem, r_sem, s, use):
        for c in range(mine):
            for p in range(SUB):
                for d in range(2):
                    if s < last(d, p):
                        ring_copy(part_of, s_sem, r_sem, d, s, c, p, True).wait_recv()
                        if s + 1 < last(d, p):
                            begin(ring_copy(part_of, s_sem, r_sem, d, s + 1, c, p))
            for d in range(2 if s < half - 1 else 1):
                use(d, s, c)

    for r in range(2, rounds - 1):
        trial_round(r)
    for k in range(1, groups):
        mig_arrival(k).wait_recv()
    for k in range(per_group):
        src = source[group * per_group + k]
        origin = lax.div(src, per_group)
        rank = jnp.int32(0)
        for j in range(k):
            other = lax.div(source[group * per_group + j], per_group)
            rank = rank + (other == origin).astype(jnp.int32)
        migrated[k] = arrived[origin * capacity + rank]

    def own_rows(owner):
        start = pl.multiple_of(z * block + owner * rows, rows)
        return pl.ds(start, rows)

    def wy_copy(k, owner):
        to = lax.rem(y + k, Y)
        return send(migrated.at[pl.ds(to * mine, mine)], walker_all.at[:, own_rows(owner)],
                    wy_s.at[k], wy_r.at[k], {"chol": at_y(k)})

    for k in range(1, Y):
        begin(wy_copy(k, y))
    for c in range(mine):
        walker_all[c, own_rows(y)] = migrated[y * mine + c]
    for r in range(max(rounds - 1, 2), rounds):
        trial_round(r)
    for k in range(1, Y):
        wy_copy(k, of_y(k)).wait_recv()
    for c in range(mine):
        ring_start(walker_part, rw_s, rw_r, c, range(SUB))
    trial_rest()
    for k in range(1, LINE):
        begin(tx_copy(k, seat))

    def turn_trial(o, carry):
        rows_here = trial_all[pl.ds(o * (Y // LINE), Y // LINE)].reshape(block, electrons)
        trial_turned[o] = rows_here.astype(F32).T.astype(BF16)
        return carry

    def trial_times(origin, c):
        return jnp.dot(trial_turned[origin], walker_all[c, block_rows(origin)],
                       preferred_element_type=F32)

    pending = []

    def add_overlap(d, s, c):
        if s < turn_at:
            pending.append((d, s, c))
        else:
            overlap[c] += trial_times(forward(signs[d], s + 1), c)

    turn_at = half - 1
    for s in range(half):
        if s == turn_at:
            for k in range(1, LINE):
                tx_copy(k, lax.rem(seat - k + LINE, LINE)).wait_recv()
            lax.fori_loop(0, depth, turn_trial, 0)
            for c in range(mine):
                overlap[c] = trial_times(z, c)
            for d, before, c in pending:
                overlap[c] += trial_times(forward(signs[d], before + 1), c)
        ring_step(walker_part, rw_s, rw_r, s, add_overlap)

    row_id = lax.broadcasted_iota(jnp.int32, (electrons, electrons), 0)
    col_id = lax.broadcasted_iota(jnp.int32, (electrons, electrons), 1)
    identity = (row_id == col_id).astype(F32)
    for c in range(mine):
        residual = identity - overlap[c]
        squared = split_dot(residual, residual)
        fourth = split_dot(squared, squared)
        low = identity + residual
        low = low + split_dot(low, squared)
        inverse = (low + split_dot(low, fourth)).astype(BF16)
        made = jnp.dot(walker_all[c, block_rows(z)], inverse, preferred_element_type=F32)
        greens_out[c] = made.astype(BF16).reshape(Y, rows, electrons)

    def turn_copy(src, dst, s_sem, r_sem, k, owner):
        to = lax.rem(y + k, Y)
        return send(src.at[:, to], dst.at[pl.ds(owner * mine, mine)],
                    s_sem.at[k], r_sem.at[k], {"chol": at_y(k)})

    for k in range(1, Y):
        begin(turn_copy(greens_out, greens_in, g_s, g_r, k, y))
    for c in range(mine):
        greens_in[y * mine + c] = greens_out[c, y]
    rot_copy.wait()
    for k in range(1, Y):
        turn_copy(greens_out, greens_in, g_s, g_r, k, of_y(k)).wait_recv()

    wide = vectors * rows
    spread = lax.dot_general(
        greens_in[...].reshape(per_group * rows, electrons), rotated_here[...],
        (((1,), (1,)), ((), ())), preferred_element_type=F32,
    )
    same_row = (lax.rem(lax.broadcasted_iota(jnp.int32, (per_group * rows, wide), 0), rows)
                == lax.rem(lax.broadcasted_iota(jnp.int32, (per_group * rows, wide), 1), rows))
    picked = jnp.where(same_row, spread, 0.0).reshape(per_group, rows, wide).sum(axis=1)
    lanes = bias_out.shape[1]
    fold = (lax.div(lax.broadcasted_iota(jnp.int32, (wide, lanes), 0), rows)
            == lax.broadcasted_iota(jnp.int32, (wide, lanes), 1)).astype(F32)
    bias_out[...] = jnp.dot(picked, fold, precision=lax.Precision.HIGHEST,
                            preferred_element_type=F32)

    def fy_copy(k, owner):
        return send(bias_out, bias_y.at[owner], fy_s.at[k], fy_r.at[k], {"chol": at_y(k)})

    for k in range(1, Y):
        begin(fy_copy(k, y))
    bias_y[y] = bias_out[...]
    for k in range(1, Y):
        fy_copy(k, of_y(k)).wait_recv()
    bias_sum[...] = bias_y[...].sum(axis=0)

    def fz_copy(k, owner):
        return send(bias_sum, bias_z.at[owner], fz_s.at[k], fz_r.at[k], {"chol": at_z(k)})

    for k in range(1, depth):
        begin(fz_copy(k, z))
    bias_z[z] = bias_sum[...]
    for k in range(1, depth):
        fz_copy(k, lax.rem(z - k + depth, depth)).wait_recv()
    total = TAU_ROOT * bias_z[...].sum(axis=0)[:, :vectors]
    force_bias[...] = total
    shifted = (fields[...] - total).astype(BF16)

    span = vectors * strip
    unfold = (lax.broadcasted_iota(jnp.int32, (vectors, span), 0)
              == lax.div(lax.broadcasted_iota(jnp.int32, (vectors, span), 1), strip)).astype(BF16)
    stretched = jnp.dot(shifted, unfold, preferred_element_type=F32)
    stretched = jnp.broadcast_to(stretched[:, None, :], (per_group, strip, span))
    kept = (lax.rem(lax.broadcasted_iota(jnp.int32, (per_group * strip, span), 0), strip)
            == lax.rem(lax.broadcasted_iota(jnp.int32, (per_group * strip, span), 1), strip))
    mixing[...] = jnp.where(kept, stretched.reshape(per_group * strip, span), 0.0).astype(BF16)

    chol_copy.wait()
    width = orbitals // CHUNKS

    def pot_copy(k, h, n, owner):
        to = lax.rem(y + k, Y)
        cols = pl.ds(n * width, width)
        return send(pot_out.at[h, pl.ds(to * mine, mine), :, cols],
                    pot_in.at[:, h, owner, :, cols],
                    p_s.at[k, h, n], p_r.at[k, h, n], {"chol": at_y(k)})

    for h in range(2):
        for n in range(CHUNKS):
            cols = pl.ds(n * width, width)
            side = chol_here[:, pl.ds(h * strip, strip), cols].reshape(span, width)
            made = TAU_ROOT * jnp.dot(mixing[...], side, preferred_element_type=F32)
            pot_out[h, :, :, cols] = made.astype(BF16).reshape(per_group, strip, width)
            for k in range(1, Y):
                begin(pot_copy(k, h, n, y))
            for c in range(mine):
                pot_in[c, h, y, :, cols] = pot_out[h, y * mine + c, :, cols]

    def first_part(origin, c, p):
        h, q = p // (SUB // 2), p % (SUB // 2)
        seats = Y // (SUB // 2)
        return first_all.at[c, origin, pl.ds(q * seats, seats), pl.ds(h * strip, strip)]

    for h in range(2):
        for n in range(CHUNKS):
            for k in range(1, Y):
                pot_copy(k, h, n, of_y(k)).wait_recv()
        for c in range(mine):
            made = jnp.dot(pot_in[c, h].reshape(Y * strip, orbitals), walker_all[c],
                           preferred_element_type=F32)
            first_f32[c, h] = made
            first_all[c, z, :, pl.ds(h * strip, strip)] = (
                made.astype(BF16).reshape(Y, strip, electrons))
            ring_start(first_part, rf_s, rf_r, c, range(h * (SUB // 2), (h + 1) * (SUB // 2)))

    def potential_times(origin, c):
        cols = pl.ds(pl.multiple_of(origin * block, block), block)
        return jnp.dot(pot_in[c, :, :, :, cols].reshape(block, block),
                       first_all[c, origin].reshape(block, electrons),
                       preferred_element_type=F32)

    def add_second(d, s, c):
        second[c] += potential_times(forward(signs[d], s + 1), c)

    for c in range(mine):
        second[c] = potential_times(z, c)
    for s in range(half):
        ring_step(first_part, rf_s, rf_r, s, add_second)

    for c in range(mine):
        own = walker_all[c, block_rows(z)].reshape(Y, rows, electrons)
        for h in range(2):
            low = own[:, h * strip:(h + 1) * strip].reshape(Y * strip, electrons).astype(F32)
            made = low + first_f32[c, h] + 0.5 * second[c, pl.ds(h * Y * strip, Y * strip)]
            result_out[c, :, pl.ds(h * strip, strip)] = (
                made.astype(BF16).reshape(Y, strip, electrons))
    for k in range(1, Y):
        begin(turn_copy(result_out, result_in, o_s, o_r, k, y))
    for c in range(mine):
        result_in[y * mine + c] = result_out[c, y]

    for k in range(1, Y):
        turn_copy(result_out, result_in, o_s, o_r, k, of_y(k)).wait_recv()
    for copy in sent:
        copy.wait_send()
    propagated[...] = result_in[...]


def shards(walkers, trial, cholesky, rotated, fields, source):
    per_group, rows, electrons = walkers.shape
    vectors = rotated.shape[0]
    groups = lax.axis_size("walk")
    depth = lax.axis_size("chol") // Y
    orbitals = cholesky.shape[2]
    capacity = per_group // 2
    mine = per_group // Y
    block = rows * Y
    half = depth // 2
    strip = rows // 2
    wide = vectors * rows
    lanes = 128
    vmem = pltpu.VMEM
    dma = pltpu.SemaphoreType.DMA
    scratch = [
        pltpu.SMEM(source.shape, jnp.int32),
        vmem(walkers.shape, BF16),
        vmem(trial.shape, BF16),
        vmem(fields.shape, F32),
        vmem((groups, capacity, rows, electrons), BF16),
        vmem((groups * capacity, rows, electrons), BF16),
        vmem((per_group, rows, electrons), BF16),
        vmem((depth * Y // LINE, LINE, rows, electrons), BF16),
        vmem((depth, electrons, block), BF16),
        vmem((mine, orbitals, electrons), BF16),
        vmem((mine, electrons, electrons), F32),
        vmem((mine, Y, rows, electrons), BF16),
        vmem((per_group, rows, electrons), BF16),
        vmem((wide, electrons), BF16),
        vmem((vectors, rows, orbitals), BF16),
        vmem((per_group, lanes), F32),
        vmem((Y, per_group, lanes), F32),
        vmem((per_group, lanes), F32),
        vmem((depth, per_group, lanes), F32),
        vmem((per_group * strip, vectors * strip), BF16),
        vmem((2, per_group, strip, orbitals), BF16),
        vmem((mine, 2, Y, strip, orbitals), BF16),
        vmem((mine, depth, Y, rows, electrons), BF16),
        vmem((mine, 2, Y * strip, electrons), F32),
        vmem((mine, block, electrons), F32),
        vmem((mine, Y, rows, electrons), BF16),
        vmem((per_group, rows, electrons), BF16),
        dma((6,)),
        dma((groups,)), dma((groups,)),
        dma((2, depth * Y // LINE // 2)), dma((2, depth * Y // LINE // 2)),
        dma((LINE,)), dma((LINE,)),
        dma((Y,)), dma((Y,)),
        dma((2, half, mine * SUB)), dma((2, half, mine * SUB)),
        dma((Y,)), dma((Y,)), dma((Y,)), dma((Y,)),
        dma((depth,)), dma((depth,)),
        dma((Y, 2, CHUNKS)), dma((Y, 2, CHUNKS)),
        dma((2, half, mine * SUB)), dma((2, half, mine * SUB)),
        dma((Y,)), dma((Y,)),
    ]
    in_vmem = pl.BlockSpec(memory_space=pltpu.VMEM)
    in_hbm = pl.BlockSpec(memory_space=pltpu.HBM)
    return pl.pallas_call(
        functools.partial(kernel, groups, depth),
        out_shape=(
            jax.ShapeDtypeStruct(walkers.shape, BF16),
            jax.ShapeDtypeStruct(fields.shape, F32),
        ),
        in_specs=[in_hbm] * 6,
        out_specs=(in_vmem, in_vmem),
        scratch_shapes=scratch,
        compiler_params=pltpu.CompilerParams(
            collective_id=0, has_side_effects=True, vmem_limit_bytes=50 * 1024 * 1024
        ),
    )(*(pltpu.with_memory_space_constraint(a, pltpu.HBM) for a in (
        source, walkers, trial, fields, rotated.reshape(wide, electrons), cholesky)))


def solution(mesh):
    placed = (
        P("walk", "chol", None),
        P("chol", None),
        P(None, "chol", None),
        P(None, "chol", None),
        P("walk", None),
        P(),
    )
    return jax.shard_map(
        shards,
        mesh=mesh,
        in_specs=placed,
        out_specs=(P("walk", "chol", None), P("walk", None)),
        check_vma=False,
    )
```

```python
import functools

import jax
import jax.numpy as jnp
from jax import lax
from jax.experimental import pallas as pl
from jax.experimental.pallas import tpu as pltpu
from jax.sharding import PartitionSpec as P

TAU_ROOT = 0.1
Y = 8
LINE = 4
CHUNKS = 2
SUB = 4
FAR_GROUPS = (4, 3, 5, 2, 6, 1, 7)
FAR_SEATS = (2, 6, 1, 3, 5, 7, 4)
F32 = jnp.float32
BF16 = jnp.bfloat16


def split_dot(a, b):
    a_hi = a.astype(BF16)
    b_hi = b.astype(BF16)
    a_lo = (a - a_hi.astype(F32)).astype(BF16)
    b_lo = (b - b_hi.astype(F32)).astype(BF16)
    dot = functools.partial(jnp.dot, preferred_element_type=F32)
    return dot(a_hi, b_hi) + (dot(a_hi, b_lo) + dot(a_lo, b_hi))


def kernel(
    groups, depth,
    source_far, walkers_far, trial_far, fields_far, rotated, cholesky,
    propagated, force_bias,
    source, walkers, trial, fields, staged, arrived, migrated, trial_all, trial_turned, walker_all, overlap,
    greens_out, greens_in, rotated_here, chol_here, bias_out, bias_y, bias_sum, bias_z,
    mixing, pot_out, pot_in, first_all, first_f32, second, result_out, result_in,
    local_sem, mig_s, mig_r, tz_s, tz_r, tx_s, tx_r, wy_s, wy_r, rw_s, rw_r,
    g_s, g_r, fy_s, fy_r, fz_s, fz_r, p_s, p_r, rf_s, rf_r, o_s, o_r,
):
    per_group, rows, electrons = walkers.shape
    vectors = fields.shape[1]
    orbitals = depth * Y * rows
    capacity = per_group // 2
    mine = per_group // Y
    block = rows * Y
    half = depth // 2
    strip = rows // 2
    group = lax.axis_index("walk")
    place = lax.axis_index("chol")
    z = lax.div(place, Y)
    y = lax.rem(place, Y)

    def at_y(k):
        return z * Y + lax.rem(y + k, Y)

    floors = depth * Y // LINE
    floor = lax.div(place, LINE)
    seat = lax.rem(place, LINE)

    def at_floor(k):
        return lax.rem(floor + k + floors, floors) * LINE + seat

    def at_z(k):
        return lax.rem(z + k + depth, depth) * Y + y

    def send(src, dst, s_sem, r_sem, where):
        return pltpu.make_async_remote_copy(
            src_ref=src, dst_ref=dst, send_sem=s_sem, recv_sem=r_sem,
            device_id=where, device_id_type=pl.DeviceIdType.MESH,
        )

    source_copy = pltpu.make_async_copy(source_far, source, local_sem.at[2])
    walkers_copy = pltpu.make_async_copy(walkers_far, walkers, local_sem.at[3])
    trial_copy = pltpu.make_async_copy(trial_far, trial, local_sem.at[4])
    fields_copy = pltpu.make_async_copy(fields_far, fields, local_sem.at[5])
    sent = []

    def begin(copy):
        copy.start()
        sent.append(copy)

    chol_copy = pltpu.make_async_copy(cholesky, chol_here, local_sem.at[0])
    rot_copy = pltpu.make_async_copy(rotated, rotated_here, local_sem.at[1])
    for copy in (source_copy, walkers_copy, trial_copy, fields_copy, rot_copy, chol_copy):
        copy.start()

    barrier = pltpu.get_barrier_semaphore()
    for k in range(1, groups):
        pl.semaphore_signal(barrier, inc=1, device_id={"walk": lax.rem(group + k, groups)},
                            device_id_type=pl.DeviceIdType.MESH)
    for k in range(1, Y):
        pl.semaphore_signal(barrier, inc=1, device_id={"chol": at_y(k)},
                            device_id_type=pl.DeviceIdType.MESH)
    for k in (1, -1):
        pl.semaphore_signal(barrier, inc=1, device_id={"chol": at_z(k)},
                            device_id_type=pl.DeviceIdType.MESH)
        pl.semaphore_signal(barrier, inc=1, device_id={"chol": at_floor(k)},
                            device_id_type=pl.DeviceIdType.MESH)

    source_copy.wait()
    walkers_copy.wait()
    trial_copy.wait()
    fields_copy.wait()

    def picks(dest):
        chosen = [jnp.int32(0)] * capacity
        count = jnp.int32(0)
        for s in range(per_group):
            src = source[dest * per_group + s]
            here = lax.div(src, per_group) == group
            slot = lax.rem(src, per_group)
            for c in range(capacity):
                chosen[c] = jnp.where(here & (count == c), slot, chosen[c])
            count = count + here.astype(jnp.int32)
        return chosen

    for k in range(1, groups):
        dest = lax.rem(group + k, groups)
        for c, pick in enumerate(picks(dest)):
            staged[k, c] = walkers[pick]
    for c, pick in enumerate(picks(group)):
        arrived[group * capacity + c] = walkers[pick]

    pl.semaphore_wait(barrier, groups + Y + 2)

    def mig_copy(k):
        dest = lax.rem(group + k, groups)
        return send(staged.at[k], arrived.at[pl.ds(group * capacity, capacity)],
                    mig_s.at[k], mig_r.at[k], {"walk": dest})

    def mig_arrival(k):
        origin = lax.rem(group - k + groups, groups)
        return send(staged.at[k], arrived.at[pl.ds(origin * capacity, capacity)],
                    mig_s.at[k], mig_r.at[k], {"walk": origin})

    signs = (1, -1)
    reach = (floors // 2, floors // 2 - 1)

    def tz_copy(d, q, arriving=False):
        hop = 1 if q % 2 else 2
        origin = lax.rem(floor - signs[d] * (q if arriving else q - hop) + 2 * floors, floors)
        part = trial_all.at[origin, seat]
        return send(part, part, tz_s.at[d, q - 1], tz_r.at[d, q - 1],
                    {"chol": at_floor(signs[d] * hop)})

    def trial_round(r):
        for d in range(2):
            if r > 0 and 2 * r <= reach[d]:
                tz_copy(d, 2 * r, True).wait_recv()
            for q in (2 * r + 2, 2 * r + 1):
                if q <= reach[d]:
                    begin(tz_copy(d, q))

    rounds = (floors // 2 + 1) // 2

    def trial_rest():
        for d in range(2):
            for q in range(1, reach[d] + 1):
                if q % 2 or q >= 2 * rounds:
                    tz_copy(d, q, True).wait_recv()

    def tx_copy(k, owner):
        part = trial_all.at[:, owner]
        return send(part, part, tx_s.at[k], tx_r.at[k],
                    {"chol": floor * LINE + lax.rem(seat + k, LINE)})

    trial_all[floor, seat] = trial[...]
    trial_round(0)
    for k in FAR_GROUPS:
        begin(mig_copy(k))
    trial_round(1)

    def of_y(k):
        return lax.rem(y - k + Y, Y)

    def rows_of(owner):
        return pl.ds(pl.multiple_of(owner * rows, rows), rows)

    def forward(k, s):
        return lax.rem(z - k * s + 2 * depth, depth)

    def block_rows(origin):
        return pl.ds(pl.multiple_of(origin * block, block), block)

    piece = block // SUB

    def last(d, p):
        return half if p % 2 == d else half - 1

    def walker_part(origin, c, p):
        return walker_all.at[c, pl.ds(pl.multiple_of(origin * block + p * piece, piece), piece)]

    def ring_copy(part_of, s_sem, r_sem, d, s, c, p, arriving=False):
        part = part_of(forward(signs[d], s + 1 if arriving else s), c, p)
        at = c * SUB + p
        return send(part, part, s_sem.at[d, s, at], r_sem.at[d, s, at],
                    {"chol": at_z(signs[d])})

    def ring_start(part_of, s_sem, r_sem, c, pieces):
        for p in pieces:
            for d in range(2):
                if last(d, p) > 0:
                    begin(ring_copy(part_of, s_sem, r_sem, d, 0, c, p))

    def ring_step(part_of, s_sem, r_sem, s, use):
        for c in range(mine):
            for p in range(SUB):
                for d in range(2):
                    if s < last(d, p):
                        ring_copy(part_of, s_sem, r_sem, d, s, c, p, True).wait_recv()
                        if s + 1 < last(d, p):
                            begin(ring_copy(part_of, s_sem, r_sem, d, s + 1, c, p))
            for d in range(2 if s < half - 1 else 1):
                use(d, s, c)

    for r in range(2, rounds - 1):
        trial_round(r)
    for k in range(1, groups):
        mig_arrival(k).wait_recv()
    for k in range(per_group):
        src = source[group * per_group + k]
        origin = lax.div(src, per_group)
        rank = jnp.int32(0)
        for j in range(k):
            other = lax.div(source[group * per_group + j], per_group)
            rank = rank + (other == origin).astype(jnp.int32)
        migrated[k] = arrived[origin * capacity + rank]

    def own_rows(owner):
        start = pl.multiple_of(z * block + owner * rows, rows)
        return pl.ds(start, rows)

    def wy_copy(k, owner):
        to = lax.rem(y + k, Y)
        return send(migrated.at[pl.ds(to * mine, mine)], walker_all.at[:, own_rows(owner)],
                    wy_s.at[k], wy_r.at[k], {"chol": at_y(k)})

    for k in FAR_SEATS:
        begin(wy_copy(k, y))
    for c in range(mine):
        walker_all[c, own_rows(y)] = migrated[y * mine + c]
    for r in range(max(rounds - 1, 2), rounds):
        trial_round(r)
    for k in range(1, Y):
        wy_copy(k, of_y(k)).wait_recv()
    for c in range(mine):
        ring_start(walker_part, rw_s, rw_r, c, range(SUB))
    trial_rest()
    for k in range(1, LINE):
        begin(tx_copy(k, seat))

    def turn_trial(o, carry):
        rows_here = trial_all[pl.ds(o * (Y // LINE), Y // LINE)].reshape(block, electrons)
        trial_turned[o] = rows_here.astype(F32).T.astype(BF16)
        return carry

    def trial_times(origin, c):
        return jnp.dot(trial_turned[origin], walker_all[c, block_rows(origin)],
                       preferred_element_type=F32)

    pending = []

    def add_overlap(d, s, c):
        if s < turn_at:
            pending.append((d, s, c))
        else:
            overlap[c] += trial_times(forward(signs[d], s + 1), c)

    turn_at = half - 1
    for s in range(half):
        if s == turn_at:
            for k in range(1, LINE):
                tx_copy(k, lax.rem(seat - k + LINE, LINE)).wait_recv()
            lax.fori_loop(0, depth, turn_trial, 0)
            for c in range(mine):
                overlap[c] = trial_times(z, c)
            for d, before, c in pending:
                overlap[c] += trial_times(forward(signs[d], before + 1), c)
        ring_step(walker_part, rw_s, rw_r, s, add_overlap)

    row_id = lax.broadcasted_iota(jnp.int32, (electrons, electrons), 0)
    col_id = lax.broadcasted_iota(jnp.int32, (electrons, electrons), 1)
    identity = (row_id == col_id).astype(F32)
    for c in range(mine):
        residual = identity - overlap[c]
        squared = split_dot(residual, residual)
        fourth = split_dot(squared, squared)
        low = identity + residual
        low = low + split_dot(low, squared)
        inverse = (low + split_dot(low, fourth)).astype(BF16)
        made = jnp.dot(walker_all[c, block_rows(z)], inverse, preferred_element_type=F32)
        greens_out[c] = made.astype(BF16).reshape(Y, rows, electrons)

    def turn_copy(src, dst, s_sem, r_sem, k, owner):
        to = lax.rem(y + k, Y)
        return send(src.at[:, to], dst.at[pl.ds(owner * mine, mine)],
                    s_sem.at[k], r_sem.at[k], {"chol": at_y(k)})

    for k in FAR_SEATS:
        begin(turn_copy(greens_out, greens_in, g_s, g_r, k, y))
    for c in range(mine):
        greens_in[y * mine + c] = greens_out[c, y]
    rot_copy.wait()
    for k in range(1, Y):
        turn_copy(greens_out, greens_in, g_s, g_r, k, of_y(k)).wait_recv()

    wide = vectors * rows
    spread = lax.dot_general(
        greens_in[...].reshape(per_group * rows, electrons), rotated_here[...],
        (((1,), (1,)), ((), ())), preferred_element_type=F32,
    )
    same_row = (lax.rem(lax.broadcasted_iota(jnp.int32, (per_group * rows, wide), 0), rows)
                == lax.rem(lax.broadcasted_iota(jnp.int32, (per_group * rows, wide), 1), rows))
    picked = jnp.where(same_row, spread, 0.0).reshape(per_group, rows, wide).sum(axis=1)
    lanes = bias_out.shape[1]
    fold = (lax.div(lax.broadcasted_iota(jnp.int32, (wide, lanes), 0), rows)
            == lax.broadcasted_iota(jnp.int32, (wide, lanes), 1)).astype(F32)
    bias_out[...] = jnp.dot(picked, fold, precision=lax.Precision.HIGHEST,
                            preferred_element_type=F32)

    def fy_copy(k, owner):
        return send(bias_out, bias_y.at[owner], fy_s.at[k], fy_r.at[k], {"chol": at_y(k)})

    for k in range(1, Y):
        begin(fy_copy(k, y))
    bias_y[y] = bias_out[...]
    for k in range(1, Y):
        fy_copy(k, of_y(k)).wait_recv()
    bias_sum[...] = bias_y[...].sum(axis=0)

    def fz_copy(k, owner):
        return send(bias_sum, bias_z.at[owner], fz_s.at[k], fz_r.at[k], {"chol": at_z(k)})

    for k in range(1, depth):
        begin(fz_copy(k, z))
    bias_z[z] = bias_sum[...]
    for k in range(1, depth):
        fz_copy(k, lax.rem(z - k + depth, depth)).wait_recv()
    total = TAU_ROOT * bias_z[...].sum(axis=0)[:, :vectors]
    force_bias[...] = total
    shifted = (fields[...] - total).astype(BF16)

    span = vectors * strip
    unfold = (lax.broadcasted_iota(jnp.int32, (vectors, span), 0)
              == lax.div(lax.broadcasted_iota(jnp.int32, (vectors, span), 1), strip)).astype(BF16)
    stretched = jnp.dot(shifted, unfold, preferred_element_type=F32)
    stretched = jnp.broadcast_to(stretched[:, None, :], (per_group, strip, span))
    kept = (lax.rem(lax.broadcasted_iota(jnp.int32, (per_group * strip, span), 0), strip)
            == lax.rem(lax.broadcasted_iota(jnp.int32, (per_group * strip, span), 1), strip))
    mixing[...] = jnp.where(kept, stretched.reshape(per_group * strip, span), 0.0).astype(BF16)

    chol_copy.wait()
    width = orbitals // CHUNKS

    def pot_copy(k, h, n, owner):
        to = lax.rem(y + k, Y)
        cols = pl.ds(n * width, width)
        return send(pot_out.at[h, pl.ds(to * mine, mine), :, cols],
                    pot_in.at[:, h, owner, :, cols],
                    p_s.at[k, h, n], p_r.at[k, h, n], {"chol": at_y(k)})

    for h in range(2):
        for n in range(CHUNKS):
            cols = pl.ds(n * width, width)
            side = chol_here[:, pl.ds(h * strip, strip), cols].reshape(span, width)
            made = TAU_ROOT * jnp.dot(mixing[...], side, preferred_element_type=F32)
            pot_out[h, :, :, cols] = made.astype(BF16).reshape(per_group, strip, width)
            for k in FAR_SEATS:
                begin(pot_copy(k, h, n, y))
            for c in range(mine):
                pot_in[c, h, y, :, cols] = pot_out[h, y * mine + c, :, cols]

    def first_part(origin, c, p):
        h, q = p // (SUB // 2), p % (SUB // 2)
        seats = Y // (SUB // 2)
        return first_all.at[c, origin, pl.ds(q * seats, seats), pl.ds(h * strip, strip)]

    for h in range(2):
        for n in range(CHUNKS):
            for k in range(1, Y):
                pot_copy(k, h, n, of_y(k)).wait_recv()
        for c in range(mine):
            made = jnp.dot(pot_in[c, h].reshape(Y * strip, orbitals), walker_all[c],
                           preferred_element_type=F32)
            first_f32[c, h] = made
            first_all[c, z, :, pl.ds(h * strip, strip)] = (
                made.astype(BF16).reshape(Y, strip, electrons))
            ring_start(first_part, rf_s, rf_r, c, range(h * (SUB // 2), (h + 1) * (SUB // 2)))

    def potential_times(origin, c):
        cols = pl.ds(pl.multiple_of(origin * block, block), block)
        return jnp.dot(pot_in[c, :, :, :, cols].reshape(block, block),
                       first_all[c, origin].reshape(block, electrons),
                       preferred_element_type=F32)

    def add_second(d, s, c):
        second[c] += potential_times(forward(signs[d], s + 1), c)

    for c in range(mine):
        second[c] = potential_times(z, c)
    for s in range(half):
        ring_step(first_part, rf_s, rf_r, s, add_second)

    for c in range(mine):
        own = walker_all[c, block_rows(z)].reshape(Y, rows, electrons)
        for h in range(2):
            low = own[:, h * strip:(h + 1) * strip].reshape(Y * strip, electrons).astype(F32)
            made = low + first_f32[c, h] + 0.5 * second[c, pl.ds(h * Y * strip, Y * strip)]
            result_out[c, :, pl.ds(h * strip, strip)] = (
                made.astype(BF16).reshape(Y, strip, electrons))
    for k in FAR_SEATS:
        begin(turn_copy(result_out, result_in, o_s, o_r, k, y))
    for c in range(mine):
        result_in[y * mine + c] = result_out[c, y]

    for k in range(1, Y):
        turn_copy(result_out, result_in, o_s, o_r, k, of_y(k)).wait_recv()
    for copy in sent:
        copy.wait_send()
    propagated[...] = result_in[...]


def shards(walkers, trial, cholesky, rotated, fields, source):
    per_group, rows, electrons = walkers.shape
    vectors = rotated.shape[0]
    groups = lax.axis_size("walk")
    depth = lax.axis_size("chol") // Y
    orbitals = cholesky.shape[2]
    capacity = per_group // 2
    mine = per_group // Y
    block = rows * Y
    half = depth // 2
    strip = rows // 2
    wide = vectors * rows
    lanes = 128
    vmem = pltpu.VMEM
    dma = pltpu.SemaphoreType.DMA
    scratch = [
        pltpu.SMEM(source.shape, jnp.int32),
        vmem(walkers.shape, BF16),
        vmem(trial.shape, BF16),
        vmem(fields.shape, F32),
        vmem((groups, capacity, rows, electrons), BF16),
        vmem((groups * capacity, rows, electrons), BF16),
        vmem((per_group, rows, electrons), BF16),
        vmem((depth * Y // LINE, LINE, rows, electrons), BF16),
        vmem((depth, electrons, block), BF16),
        vmem((mine, orbitals, electrons), BF16),
        vmem((mine, electrons, electrons), F32),
        vmem((mine, Y, rows, electrons), BF16),
        vmem((per_group, rows, electrons), BF16),
        vmem((wide, electrons), BF16),
        vmem((vectors, rows, orbitals), BF16),
        vmem((per_group, lanes), F32),
        vmem((Y, per_group, lanes), F32),
        vmem((per_group, lanes), F32),
        vmem((depth, per_group, lanes), F32),
        vmem((per_group * strip, vectors * strip), BF16),
        vmem((2, per_group, strip, orbitals), BF16),
        vmem((mine, 2, Y, strip, orbitals), BF16),
        vmem((mine, depth, Y, rows, electrons), BF16),
        vmem((mine, 2, Y * strip, electrons), F32),
        vmem((mine, block, electrons), F32),
        vmem((mine, Y, rows, electrons), BF16),
        vmem((per_group, rows, electrons), BF16),
        dma((6,)),
        dma((groups,)), dma((groups,)),
        dma((2, depth * Y // LINE // 2)), dma((2, depth * Y // LINE // 2)),
        dma((LINE,)), dma((LINE,)),
        dma((Y,)), dma((Y,)),
        dma((2, half, mine * SUB)), dma((2, half, mine * SUB)),
        dma((Y,)), dma((Y,)), dma((Y,)), dma((Y,)),
        dma((depth,)), dma((depth,)),
        dma((Y, 2, CHUNKS)), dma((Y, 2, CHUNKS)),
        dma((2, half, mine * SUB)), dma((2, half, mine * SUB)),
        dma((Y,)), dma((Y,)),
    ]
    in_vmem = pl.BlockSpec(memory_space=pltpu.VMEM)
    in_hbm = pl.BlockSpec(memory_space=pltpu.HBM)
    return pl.pallas_call(
        functools.partial(kernel, groups, depth),
        out_shape=(
            jax.ShapeDtypeStruct(walkers.shape, BF16),
            jax.ShapeDtypeStruct(fields.shape, F32),
        ),
        in_specs=[in_hbm] * 6,
        out_specs=(in_vmem, in_vmem),
        scratch_shapes=scratch,
        compiler_params=pltpu.CompilerParams(
            collective_id=0, has_side_effects=True, vmem_limit_bytes=50 * 1024 * 1024
        ),
    )(*(pltpu.with_memory_space_constraint(a, pltpu.HBM) for a in (
        source, walkers, trial, fields, rotated.reshape(wide, electrons), cholesky)))


def solution(mesh):
    placed = (
        P("walk", "chol", None),
        P("chol", None),
        P(None, "chol", None),
        P(None, "chol", None),
        P("walk", None),
        P(),
    )
    return jax.shard_map(
        shards,
        mesh=mesh,
        in_specs=placed,
        out_specs=(P("walk", "chol", None), P("walk", None)),
        check_vma=False,
    )
```
